128 devices in a mesh: dp: 4 (over x), fsdp: 32 (over z, y, core).
Axes of the slice: x: 4, y: 4, z: 4, core: 2. Of those that a mesh axis runs over, the one named last changes fastest.
Arguments:
- tokens: bfloat16 [65536, 8192], P(('dp', 'fsdp')), may hold values from -6 to 6
- cotangent: bfloat16 [65536, 1024], P(('dp', 'fsdp')), may hold values from -0.023925781 to 0.023925781
- base_weight: bfloat16 [8192, 1024], P('fsdp'), may hold values from -0.0625 to 0.0625
- deltas: bfloat16 [128, 128, 128], P('fsdp'), may hold values from -0.19921875 to 0.19921875
- tile_rows: int32 [128], replicated, may hold values from 0 to 63, as said below
- tile_cols: int32 [128], replicated, may hold values from 0 to 7, as said below
- used: int32 [32], replicated, may hold values from 1 to 4, as said below
Outputs:
- values: bfloat16 [65536, 1024], P(('dp', 'fsdp'))
- delta_grad: float32 [128, 128, 128], P('fsdp')
The draws below stay inside these ranges and needn't reach their ends.
Inputs may be any that keep to these rules, and one draw needn't show every extreme that they name: The pairs (tile_rows[s], tile_cols[s]) over all 128 slots are distinct. `tile_cols`: see tile_rows. `used`: some owner has all 4 slots live.
All inputs are finite; a program needn't handle non-finite values.
Results may differ from the reference program's by a relative error of at most 0.0043.
Values may be sent and summed in bfloat16 or wider, within the bound.
No kernel may reach another device: no remote copies, remote signals or barrier semaphores. Data moves between devices by JAX's collectives and lax.ppermute only.
A program may use at most 128 MiB of HBM per device.

```python
import jax
import jax.numpy as jnp
from jax import lax

D = 8192
KV = 1024
TILE_SIDE = 128
OWNER_SLOTS = 4
TOKENS = 65536
TOTAL_SLOTS = 128


def tile_pairs(key):
    across = KV // TILE_SIDE
    grand_total = D // TILE_SIDE * across
    slot_ordering = jax.random.permutation(jax.random.fold_in(key, 11), grand_total)[:TOTAL_SLOTS]
    return (slot_ordering // across, slot_ordering % across)


def draw_tile_rows(key, part):
    return tile_pairs(key)[0].astype(jnp.int32)


def draw_tile_cols(key, part):
    return tile_pairs(key)[1].astype(jnp.int32)


def draw_used(key, part):
    owner_list = TOTAL_SLOTS // OWNER_SLOTS
    first, second = jax.random.split(jax.random.fold_in(key, 23))
    counts = jax.random.randint(first, (owner_list,), 1, OWNER_SLOTS + 1)
    fullest = jax.random.randint(second, (), 0, owner_list)
    return jnp.where(jnp.arange(owner_list) == fullest, OWNER_SLOTS, counts).astype(jnp.int32)


def block_levels(own_key, dims, pieces, low, high):
    def one(position, blocks):
        heights = jax.random.uniform(jax.random.fold_in(jax.random.fold_in(own_key, 6), position), (blocks,), jnp.float32, low / len(pieces), high / len(pieces))
        return jnp.repeat(jnp.exp(heights), dims[position] // blocks).reshape((-1,) + (1,) * (len(dims) - position - 1))

    gain = one(*pieces[0])
    for cut in pieces[1:]:
        gain = gain * one(*cut)
    return gain


def gaussian(rng, dims, spread, reach, cuts=(), kind=jnp.bfloat16):
    loudness = block_levels(rng, dims, cuts, -0.22, 0.18) if cuts else 1.0
    entries = jax.random.normal(rng, dims, jnp.float32) * spread * loudness
    return jnp.minimum(jnp.maximum(entries, -reach), reach).astype(kind)


def setup_inputs(seed: int = 0) -> dict:
    seeds = jax.random.split(jax.random.key(seed), 8)
    tokens = gaussian(seeds[0], (TOKENS, D), 1.0, 6.0, ((0, 128),))
    cotangent = gaussian(seeds[1], (TOKENS, KV), 0.004, 0.023925781, ((0, 128),))
    base_weight = gaussian(seeds[2], (D, KV), D ** -0.5, 0.0625, ((0, 32),))
    deltas = gaussian(seeds[3], (TOTAL_SLOTS, TILE_SIDE, TILE_SIDE), 0.03, 0.19921875, ((0, 32),))
    tile_rows = draw_tile_rows(jax.random.fold_in(seeds[7], 71), 0)
    tile_cols = draw_tile_cols(jax.random.fold_in(seeds[7], 71), 0)
    used = draw_used(jax.random.fold_in(seeds[7], 71), 0)
    return {"tokens": tokens, "cotangent": cotangent, "base_weight": base_weight, "deltas": deltas, "tile_rows": tile_rows, "tile_cols": tile_cols, "used": used}


def live_slots(used, per_owner):
    slot_position = jnp.arange(used.shape[0] * per_owner, dtype=jnp.int32) % per_owner
    return slot_position < jnp.repeat(used, per_owner)


def restore_tiles(weight, tile, rows, cols, deltas, keep):
    wrows = weight.shape[0] // tile
    grid = weight.reshape(wrows, tile, weight.shape[1] // tile, tile)
    safe = jnp.clip(rows, 0, wrows - 1).astype(jnp.int32)
    old = grid[safe, :, cols, :]
    fresh = (old.astype(jnp.float32) + deltas.astype(jnp.float32)).astype(jnp.bfloat16)
    target = jnp.where(keep, rows, wrows).astype(jnp.int32)
    grid = grid.at[target, :, cols, :].set(fresh, mode="drop")
    return grid.reshape(weight.shape)


def reference(tokens, cotangent, base_weight, deltas, tile_rows, tile_cols, used):
    live = live_slots(used, OWNER_SLOTS)
    restored = restore_tiles(base_weight, TILE_SIDE, tile_rows, tile_cols, deltas, live)
    values = jnp.dot(tokens, restored, preferred_element_type=jnp.float32).astype(jnp.bfloat16)

    def one_slot(item):
        row, col, keep = item
        left = lax.dynamic_slice_in_dim(tokens, (row * TILE_SIDE).astype(jnp.int32), TILE_SIDE, 1)
        right = lax.dynamic_slice_in_dim(cotangent, (col * TILE_SIDE).astype(jnp.int32), TILE_SIDE, 1)
        block = lax.dot_general(left, right, (((0,), (0,)), ((), ())), preferred_element_type=jnp.float32)
        return block * keep.astype(jnp.float32)

    delta_grad = lax.map(one_slot, (tile_rows, tile_cols, live))
    return values, delta_grad
```

```python
import jax
import jax.numpy as jnp
from jax import lax
from jax.experimental import pallas as pl
from jax.experimental.pallas import tpu as pltpu
from jax.sharding import PartitionSpec as P


OFFS = (0, -1, 1, 2)
BF = jnp.bfloat16
F32 = jnp.float32


def dev(z, y, c):
    return ((z % 4) * 4 + y % 4) * 2 + c


def shift(x, s0, s1):
    pairs = []
    for z in range(4):
        for y in range(4):
            pairs.append((dev(z, y, 0), dev(z + s0[0], y + s0[1], 0)))
            pairs.append((dev(z, y, 1), dev(z + s1[0], y + s1[1], 1)))
    return lax.ppermute(x, "fsdp", pairs)


def swap(x):
    return lax.ppermute(x, "fsdp", [(i, i ^ 1) for i in range(32)])


def shift_x(x, d):
    return lax.ppermute(x, "dp", [(i, (i + d) % 4) for i in range(4)])


def ring_one(x):
    return [x] + [shift(x, (-o, 0), (0, -o)) for o in OFFS[1:]]


def ring_two(x):
    return [x] + [shift(x, (0, -o), (-o, 0)) for o in OFFS[1:]]


def grad_body(rows, cols, live, *refs, per):
    toks = refs[:per]
    toks2 = refs[per : 2 * per]
    cot, cot2, out = refs[2 * per :]
    i = pl.program_id(0)
    dims = (((0,), (0,)), ((), ()))
    for k in range(per):
        s = i * per + k
        c = pl.multiple_of(cols[s] * 128, 128)
        g = lax.dot_general(toks[k][...], cot[:, pl.ds(c, 128)], dims, preferred_element_type=F32)
        g = g + lax.dot_general(toks2[k][...], cot2[:, pl.ds(c, 128)], dims, preferred_element_type=F32)
        out[k] = jnp.where(live[s] > 0, g, 0.0).astype(out.dtype)


def grads(rows, cols, live, tok, tok2, cot, cot2, dtype, per=8):
    n = rows.shape[0]
    t = tok.shape[0]

    def tok_spec(k):
        return pl.BlockSpec((t, 128), lambda i, r, c, l: (0, r[i * per + k]))

    full = pl.BlockSpec((t, cot.shape[1]), lambda i, r, c, l: (0, 0), pipeline_mode=pl.Buffered(1))
    return pl.pallas_call(
        lambda *a: grad_body(*a, per=per),
        out_shape=jax.ShapeDtypeStruct((n, 128, 128), dtype),
        grid_spec=pltpu.PrefetchScalarGridSpec(
            num_scalar_prefetch=3,
            grid=(n // per,),
            in_specs=[tok_spec(k) for k in range(per)] * 2 + [full, full],
            out_specs=pl.BlockSpec((per, 128, 128), lambda i, r, c, l: (i, 0, 0)),
        ),
        name="grads",
        cost_estimate=pl.CostEstimate(flops=n * 4 * t * 128 * 128, bytes_accessed=n * 4 * t * 128, transcendentals=0),
    )(rows, cols, live, *([tok] * per), *([tok2] * per), cot, cot2)


def mm_body(kidx, table, *refs, nb, has_acc):
    ws = refs[:nb]
    tok, tok2, da, db = refs[nb : nb + 4]
    rest = refs[nb + 4 :]
    if has_acc:
        a_in, b_in, a_out, b_out, scratch = rest
    else:
        a_out, b_out, scratch = rest
    i = pl.program_id(0)
    for b in range(nb):

        @pl.when(i // 4 == b)
        def _():
            scratch[...] = ws[b][0]

    base = kidx[i] * 16

    def one(t, carry):
        p = table[base + t]
        r = pl.multiple_of((t // 8) * 128, 128)
        c = pl.multiple_of((t % 8) * 128, 128)

        @pl.when((p >= 0) & (p < 64))
        def _():
            old = scratch[pl.ds(r, 128), pl.ds(c, 128)].astype(F32)
            scratch[pl.ds(r, 128), pl.ds(c, 128)] = (old + da[jnp.minimum(p, 63)].astype(F32)).astype(BF)

        @pl.when(p >= 64)
        def _():
            old = scratch[pl.ds(r, 128), pl.ds(c, 128)].astype(F32)
            scratch[pl.ds(r, 128), pl.ds(c, 128)] = (old + db[jnp.maximum(p, 64) - 64].astype(F32)).astype(BF)

        return carry

    lax.fori_loop(0, 16, one, 0)
    w = scratch[...]
    pa = jnp.dot(tok[...], w, preferred_element_type=F32)
    pb = jnp.dot(tok2[...], w, preferred_element_type=F32)

    @pl.when(i == 0)
    def _():
        if has_acc:
            a_out[...] = a_in[...] + pa
            b_out[...] = b_in[...] + pb
        else:
            a_out[...] = pa
            b_out[...] = pb

    @pl.when(i > 0)
    def _():
        a_out[...] += pa
        b_out[...] += pb


def mm(kidx, table, bufs, tok, tok2, da, db, acc=None):
    nb = len(bufs)
    t = tok.shape[0]
    n = bufs[0].shape[2]

    def w_spec(b):
        return pl.BlockSpec((1, 256, n), lambda i, k, tb: (jnp.clip(i - 4 * b, 0, 3), 0, 0))

    tspec = pl.BlockSpec((t, 256), lambda i, k, tb: (0, k[i]))
    dspec = pl.BlockSpec((64, 128, 128), lambda i, k, tb: (0, 0, 0), pipeline_mode=pl.Buffered(1))
    ospec = pl.BlockSpec((t, n), lambda i, k, tb: (0, 0))
    args = list(bufs) + [tok, tok2, da, db] + (list(acc) if acc else [])
    specs = [w_spec(b) for b in range(nb)] + [tspec, tspec, dspec, dspec] + ([ospec, ospec] if acc else [])
    o = jax.ShapeDtypeStruct((t, n), F32)
    return pl.pallas_call(
        lambda *a: mm_body(*a, nb=nb, has_acc=bool(acc)),
        out_shape=(o, o),
        grid_spec=pltpu.PrefetchScalarGridSpec(
            num_scalar_prefetch=2,
            grid=(4 * nb,),
            in_specs=specs,
            out_specs=(ospec, ospec),
            scratch_shapes=[pltpu.VMEM((256, n), BF)],
        ),
        name="mm",
        cost_estimate=pl.CostEstimate(flops=nb * 1024 * 4 * t * n, bytes_accessed=nb * 1024 * 2 * (n + 2 * t) + 4 * t * n * 4, transcendentals=0),
    )(kidx, table, *args)


def where_in_order(d):
    d = d % 4
    return jnp.where(d == 0, 0, jnp.where(d == 3, 1, jnp.where(d == 1, 2, 3)))


def shards(tokens, cotangent, base_weight, deltas, tile_rows, tile_cols, used):
    x = lax.axis_index("dp")
    f = lax.axis_index("fsdp")
    z, y, c = f // 8, (f // 2) % 4, f % 2
    slots = jnp.arange(128, dtype=jnp.int32)
    live = ((slots % 4) < jnp.repeat(used, 4)).astype(jnp.int32)

    w_one = ring_one(base_weight)
    tok2 = swap(tokens)
    cot2 = swap(cotangent)
    d_one = ring_one(lax.dynamic_slice_in_dim(deltas, x, 1, 0))
    d_two = ring_two(jnp.concatenate(d_one))
    w_two = ring_two(jnp.stack(w_one))
    d_two = jnp.concatenate(d_two)
    d_x = jnp.concatenate([d_two] + [shift_x(d_two, -o) for o in OFFS[1:]])
    d_sw = swap(d_x)

    q = jnp.arange(16, dtype=jnp.int32)
    own = dev(z + q % 4, y + q // 4, c)
    part = []
    for d in (2, 1, 3, 0):
        ids = own * 4 + (x + d) % 4
        part.append(grads(tile_rows[ids], tile_cols[ids], live[ids], tokens, tok2, cotangent, cot2, F32 if d == 0 else BF))
    got = [shift_x(p, d) for p, d in zip(part[:3], (2, 1, 3))]
    s = [part[3][4 * k : 4 * k + 4] + sum(g[4 * k : 4 * k + 4].astype(F32) for g in got) for k in range(4)]
    t = s[0] + sum(shift(s[k], (0, k), (0, k)) for k in (1, 2, 3))
    u = t[0:1] + sum(shift(t[k : k + 1], (k, 0), (k, 0)) for k in (1, 2, 3))
    ux = [u] + [shift_x(u, k) for k in (1, 2, 3)]
    ring = jnp.concatenate(ux[::-1] + ux[::-1])
    delta_grad = lax.dynamic_slice_in_dim(ring, (3 - x) % 4, 4, 0)

    so, sj = slots // 4, slots % 4
    sz, sy, sc = so // 8, (so // 2) % 4, so % 2
    mz, my, mx = where_in_order(sz - z), where_in_order(sy - y), where_in_order(sj - x)
    a = jnp.where(sc == 0, mz, my)
    b = jnp.where(sc == 0, my, mz)
    pos = jnp.where(sc == c, 0, 64) + mx * 16 + b * 4 + a
    at = tile_rows * 8 + tile_cols
    hit = (at[None, :] == jnp.arange(512, dtype=jnp.int32)[:, None]) & (live[None, :] > 0)
    table = jnp.max(jnp.where(hit, pos[None, :], -1), axis=1)

    offs = jnp.array(OFFS, jnp.int32)
    first = jnp.tile(offs, 4)
    second = jnp.repeat(offs, 4)
    dz = jnp.where(c == 0, first, second)
    dy = jnp.where(c == 0, second, first)
    kidx = dev(z + dz, y + dy, c).astype(jnp.int32)

    acc = mm(kidx[:12], table, w_two[:3], tokens, tok2, d_x, d_sw)
    mine, theirs = mm(kidx[12:], table, w_two[3:], tokens, tok2, d_x, d_sw, acc)
    values = (mine + swap(theirs)).astype(BF)
    return values, delta_grad


def solution(mesh):
    in_specs = (
        P(("dp", "fsdp"), None),
        P(("dp", "fsdp"), None),
        P("fsdp", None),
        P("fsdp", None, None),
        P(),
        P(),
        P(),
    )
    out_specs = (P(("dp", "fsdp"), None), P("fsdp", None, None))
    return jax.shard_map(shards, mesh=mesh, in_specs=in_specs, out_specs=out_specs, check_vma=False)
```

```python
import jax
import jax.numpy as jnp
from jax import lax
from jax.experimental import pallas as pl
from jax.experimental.pallas import tpu as pltpu
from jax.sharding import PartitionSpec as P


BF = jnp.bfloat16
F32 = jnp.float32
I32 = jnp.int32
MASKS = ((1, 3), (3, 1))


def pair(x, axis, step):
    pairs = []
    if axis == "x":
        for px in range(4):
            for f in range(32):
                pairs.append((px * 32 + f, (px ^ MASKS[step][f & 1]) * 32 + f))
        return lax.ppermute(x, ("dp", "fsdp"), pairs)
    sh = 3 if axis == "z" else 1
    for f in range(32):
        pairs.append((f, f ^ (MASKS[step][f & 1] << sh)))
    return lax.ppermute(x, "fsdp", pairs)


def swap(x):
    return lax.ppermute(x, "fsdp", [(i, i ^ 1) for i in range(32)])


def gray(o):
    return o ^ (o >> 1)


def other(o):
    return jnp.where(o == 0, 0, jnp.where(o == 1, 3, o - 1))


def other_place(d):
    return jnp.where(d == 0, 0, jnp.where(d == 3, 1, d + 1))


def dev(z, y, c):
    return z * 8 + y * 2 + c


def grad_body(ids, rows, cols, used, *refs, per, base):
    toks = refs[:per]
    toks2 = refs[per : 2 * per]
    cot, cot2, out = refs[2 * per :]
    i = pl.program_id(0)
    dims = (((0,), (0,)), ((), ()))
    for k in range(per):
        s = ids[base + i * per + k]
        c = pl.multiple_of(cols[s] * 128, 128)
        g = lax.dot_general(toks[k][...], cot[:, pl.ds(c, 128)], dims, preferred_element_type=F32)
        g = g + lax.dot_general(toks2[k][...], cot2[:, pl.ds(c, 128)], dims, preferred_element_type=F32)
        on = (s & 3) < used[s >> 2]
        out[k] = jnp.where(on, g, 0.0).astype(out.dtype)


def grads(ids, base, n, rows, cols, used, tok, tok2, cot, cot2, dtype, per=8):
    t = tok.shape[0]

    def tok_spec(k):
        return pl.BlockSpec((t, 128), lambda i, d, r, c, u: (0, r[d[base + i * per + k]]))

    full = pl.BlockSpec((t, cot.shape[1]), lambda i, *_: (0, 0), pipeline_mode=pl.Buffered(1))
    return pl.pallas_call(
        lambda *a: grad_body(*a, per=per, base=base),
        out_shape=jax.ShapeDtypeStruct((n, 128, 128), dtype),
        grid_spec=pltpu.PrefetchScalarGridSpec(
            num_scalar_prefetch=4,
            grid=(n // per,),
            in_specs=[tok_spec(k) for k in range(per)] * 2 + [full, full],
            out_specs=pl.BlockSpec((per, 128, 128), lambda i, *_: (i, 0, 0)),
        ),
        compiler_params=pltpu.CompilerParams(vmem_limit_bytes=16 << 20),
        name="grads",
        cost_estimate=pl.CostEstimate(flops=n * 4 * t * 128 * 128, bytes_accessed=n * 4 * t * 128, transcendentals=0),
    )(ids, rows, cols, used, *([tok] * per), *([tok2] * per), cot, cot2)


def mm_body(krow, table, *refs, nb, base, has_acc):
    ws = refs[:nb]
    toks = refs[nb : nb + 4]
    toks2 = refs[nb + 4 : nb + 8]
    da, db = refs[nb + 8 : nb + 10]
    rest = refs[nb + 10 :]
    if has_acc:
        a_in, b_in, a_out, b_out, scratch = rest
    else:
        a_out, b_out, scratch = rest
    i = pl.program_id(0)
    for b in range(nb):

        @pl.when(i == b)
        def _():
            scratch[...] = ws[b][...].reshape(scratch.shape)

    for q in range(4):
        row = krow[base + i * 4 + q] * 8
        for j in range(8):
            p = table[row + j]

            @pl.when(p >= 0)
            def _():
                tile = (slice(128 * q, 128 * q + 128), slice(128 * j, 128 * j + 128))

                @pl.when(p < 64)
                def _():
                    scratch[tile] = (scratch[tile].astype(F32) + da[p & 63].astype(F32)).astype(BF)

                @pl.when(p >= 64)
                def _():
                    scratch[tile] = (scratch[tile].astype(F32) + db[p & 63].astype(F32)).astype(BF)

    w = scratch[...]
    ta = jnp.concatenate([r[...] for r in toks], axis=1)
    tb = jnp.concatenate([r[...] for r in toks2], axis=1)

    @pl.when(i == 0)
    def _():
        if has_acc:
            a_out[...] = a_in[...] + jnp.dot(ta, w, preferred_element_type=F32)
            b_out[...] = b_in[...] + jnp.dot(tb, w, preferred_element_type=F32)
        else:
            a_out[...] = jnp.dot(ta, w, preferred_element_type=F32)
            b_out[...] = jnp.dot(tb, w, preferred_element_type=F32)

    @pl.when(i > 0)
    def _():
        a_out[...] += jnp.dot(ta, w, preferred_element_type=F32)
        b_out[...] += jnp.dot(tb, w, preferred_element_type=F32)


def mm(krow, table, base, bufs, tok, tok2, da, db, acc=None):
    nb = len(bufs)
    t = tok.shape[0]
    n = bufs[0].shape[1]
    once = pl.Buffered(1)

    def w_spec(b):
        return pl.BlockSpec((512, n), lambda i, *_: (0, 0), pipeline_mode=once)

    def t_spec(q):
        return pl.BlockSpec((t, 128), lambda i, k, tb: (0, k[base + i * 4 + q]))

    d_spec = pl.BlockSpec((64, 128, 128), lambda i, *_: (0, 0, 0), pipeline_mode=once)
    o_spec = pl.BlockSpec((t, n), lambda i, *_: (0, 0), pipeline_mode=once)
    t_specs = [t_spec(q) for q in range(4)]
    args = list(bufs) + [tok] * 4 + [tok2] * 4 + [da, db] + (list(acc) if acc else [])
    specs = [w_spec(b) for b in range(nb)] + t_specs * 2 + [d_spec, d_spec] + ([o_spec, o_spec] if acc else [])
    o = jax.ShapeDtypeStruct((t, n), F32)
    return pl.pallas_call(
        lambda *a: mm_body(*a, nb=nb, base=base, has_acc=bool(acc)),
        out_shape=(o, o),
        grid_spec=pltpu.PrefetchScalarGridSpec(
            num_scalar_prefetch=2,
            grid=(nb,),
            in_specs=specs,
            out_specs=(o_spec, o_spec),
            scratch_shapes=[pltpu.VMEM((512, n), BF)],
        ),
        compiler_params=pltpu.CompilerParams(vmem_limit_bytes=28 << 20),
        name="mm",
        cost_estimate=pl.CostEstimate(flops=nb * 512 * 4 * t * n, bytes_accessed=nb * 512 * 2 * (n + 2 * t) + 4 * t * n * 4, transcendentals=0),
    )(krow, table, *args)


def order_body(place, u, r1, r2, out):
    for j in range(4):
        p = place[j]

        @pl.when(p == 0)
        def _():
            out[j] = u[0]

        @pl.when(p == 1)
        def _():
            out[j] = r1[0]

        @pl.when(p >= 2)
        def _():
            out[j] = r2[p & 1]


def in_order(place, u, r1, r2):
    return pl.pallas_call(
        order_body,
        out_shape=jax.ShapeDtypeStruct((4, 128, 128), F32),
        grid_spec=pltpu.PrefetchScalarGridSpec(
            num_scalar_prefetch=1,
            grid=(1,),
            in_specs=[pl.BlockSpec(v.shape, lambda i, p: (0, 0, 0)) for v in (u, r1, r2)],
            out_specs=pl.BlockSpec((4, 128, 128), lambda i, p: (0, 0, 0)),
        ),
        compiler_params=pltpu.CompilerParams(vmem_limit_bytes=8 << 20),
        name="in_order",
        cost_estimate=pl.CostEstimate(flops=0, bytes_accessed=1 << 19, transcendentals=0),
    )(place, u, r1, r2)


def shards(tokens, cotangent, base_weight, deltas, tile_rows, tile_cols, used):
    x = lax.axis_index("dp").astype(I32)
    f = lax.axis_index("fsdp").astype(I32)
    z, y, c = f >> 3, (f >> 1) & 3, f & 1
    cat = lambda *v: jnp.concatenate(v, axis=0)

    def spread(o):
        return jnp.where(c == 0, gray(o), other(o))

    def fold(o):
        return jnp.where(c == 0, other(o), gray(o))

    a0, b0 = base_weight[:128], base_weight[128:]
    tok2 = swap(tokens)
    cot2 = swap(cotangent)
    a = cat(a0, pair(a0, "z", 0))
    b = cat(b0, pair(b0, "y", 0))
    a = cat(a, pair(a, "z", 1))
    b = cat(b, pair(b, "y", 1))
    a1, b1 = pair(a, "y", 0), pair(b, "z", 0)
    a2, b2 = pair(a, "y", 1), pair(b, "z", 1)
    a3, b3 = pair(a1, "y", 1), pair(b1, "z", 1)

    d = lax.dynamic_slice_in_dim(deltas, x, 1, 0)
    for axis in ("z", "y", "x"):
        for step in (0, 1):
            d = cat(d, pair(d, axis, step))
    d2 = swap(d)

    i = lax.iota(I32, 64)
    xo = fold(((i >> 4) + 2) & 3)
    ids = dev(z ^ fold(i & 3), y ^ fold((i >> 2) & 3), c) * 4 + (x ^ xo)
    args = (tile_rows, tile_cols, used, tokens, tok2, cotangent, cot2)
    g1 = grads(ids, 0, 32, *args, BF)
    r = pair(g1, "x", 0)
    g2 = grads(ids, 32, 32, *args, F32)
    r2 = pair((g2[16:] + r[16:].astype(F32)).astype(BF), "x", 1)
    s = g2[:16] + r[:16].astype(F32) + r2.astype(F32)
    s = s[:8] + pair(s[8:], "y", 0)
    s = s[:4] + pair(s[4:], "y", 1)
    s = s[:2] + pair(s[2:], "z", 0)
    u = s[:1] + pair(s[1:], "z", 1)
    u1 = pair(u, "x", 0)
    u2 = pair(cat(u, u1), "x", 1)
    j = lax.iota(I32, 4) ^ x
    delta_grad = in_order(jnp.where(c == 0, gray(j), other_place(j)), u, u1, u2)

    slots = lax.iota(I32, 128)
    oz, oy, oc, ox = (slots >> 5) ^ z, ((slots >> 3) & 3) ^ y, (slots >> 2) & 1, (slots & 3) ^ x

    def place(v):
        return jnp.where(oc == 0, gray(v), other_place(v))

    pos = ((oc ^ c) << 6) + (place(ox) << 4) + (place(oy) << 2) + place(oz)
    live = (slots & 3) < jnp.repeat(used, 4)
    at = jnp.where(live, tile_rows * 8 + tile_cols, -1)
    hit = at[None, :] == lax.broadcasted_iota(I32, (512, 128), 0)
    table = jnp.max(jnp.where(hit, pos[None, :], -1), axis=1)

    k = lax.iota(I32, 32)
    o1, o2, fl = spread(k & 3), spread(k >> 3), (k >> 2) & 1
    krow = dev(z ^ jnp.where(fl == 0, o1, o2), y ^ jnp.where(fl == 0, o2, o1), c) * 2 + fl

    acc = mm(krow, table, 0, (a, b, a1, b1), tokens, tok2, d, d2)
    mine, theirs = mm(krow, table, 16, (a2, b2, a3, b3), tokens, tok2, d, d2, acc)
    values = (mine + swap(theirs)).astype(BF)
    return values, delta_grad


def solution(mesh):
    in_specs = (
        P(("dp", "fsdp"), None),
        P(("dp", "fsdp"), None),
        P("fsdp", None),
        P("fsdp", None, None),
        P(),
        P(),
        P(),
    )
    out_specs = (P(("dp", "fsdp"), None), P("fsdp", None, None))
    return jax.shard_map(shards, mesh=mesh, in_specs=in_specs, out_specs=out_specs, check_vma=False)
```
